32 devices in a mesh: grp: 2 (over y), dev: 16 (over z, x, core).
Axes of the slice: x: 2, y: 2, z: 4, core: 2. Of those that a mesh axis runs over, the one named last changes fastest.
Arguments:
- sources: bfloat16 [65536, 768], P(('grp', 'dev')), may hold values from -6 to 6
- encoder: bfloat16 [65536, 256], P(('grp', 'dev')), may hold values from -0.125 to 0.125
- section_weight: bfloat16 [32, 4, 2, 256, 256], P(('grp', 'dev')), may hold values from -0.25 to 0.25
- cross_weight: bfloat16 [2, 16, 2, 256, 256], P('grp', 'dev'), may hold values from -0.25 to 0.25
- local_weight: bfloat16 [32, 14, 256, 256], P(('grp', 'dev')), may hold values from -0.375 to 0.375
- decoder: bfloat16 [65536, 256], P(('grp', 'dev')), may hold values from -0.375 to 0.375
Outputs:
- target_values: bfloat16 [65536, 768], P(('grp', 'dev'))
The draws below stay inside these ranges and needn't reach their ends.
All inputs are finite; a program needn't handle non-finite values.
Results may differ from the reference program's by a relative error of at most 0.02.
Values may be sent and summed in bfloat16 or wider, within the bound.
No kernel may reach another device: no remote copies, remote signals or barrier semaphores. Data moves between devices by JAX's collectives and lax.ppermute only.
A program may use at most 64 MiB of HBM per device.

```python
import jax
import jax.numpy as jnp
import numpy as np

K = 256
R = 768
PTS_DEV = 2048
LOCAL = 3
BITS = 4
MATS = 14
LEAF_T = 256
NPTS = 65536
N_GRP = 2
N_DEV = 16


def shard_levels(key, shape, shards, smallest, high):
    factor_of = 1.0
    for dim, parts in shards:
        steps = jax.random.uniform(jax.random.fold_in(jax.random.fold_in(key, 6), dim), (parts,), jnp.float32, smallest / len(shards), high / len(shards))
        factor_of = factor_of * jnp.repeat(jnp.exp(steps), shape[dim] // parts).reshape((-1,) + (1,) * (len(shape) - 1 - dim))
    return factor_of


def scatter_about(stream_key, dims, spread, most, shards=(), kind=jnp.bfloat16):
    array = spread * jax.random.normal(stream_key, dims, jnp.float32)
    if shards:
        array = array * shard_levels(stream_key, dims, shards, -0.22, 0.18)
    return jnp.clip(array, -most, most).astype(kind)


def setup_inputs(seed: int = 0) -> dict:
    streams_of = jax.random.split(jax.random.key(seed), 7)
    sources = scatter_about(streams_of[0], (NPTS, R), 1.0, 6.0, ((0, 32),))
    encoder = scatter_about(streams_of[1], (NPTS, K), PTS_DEV ** -0.5, 0.125, ((0, 32),))
    section_weight = scatter_about(streams_of[2], (N_GRP * N_DEV, BITS, 2, K, K), (2 * K) ** -0.5, 0.25, ((0, 32),))
    cross_weight = scatter_about(streams_of[3], (N_GRP, N_DEV, N_GRP, K, K), (N_GRP * K) ** -0.5, 0.25, ((0, 2), (1, 16)))
    local_weight = scatter_about(streams_of[4], (N_GRP * N_DEV, MATS, K, K), K ** -0.5, 0.375, ((0, 32),))
    decoder = scatter_about(streams_of[5], (NPTS, K), K ** -0.5, 0.375, ((0, 32),))
    return dict(sources=sources, encoder=encoder, section_weight=section_weight, cross_weight=cross_weight, local_weight=local_weight, decoder=decoder)


def reference(sources, encoder, section_weight, cross_weight, local_weight, decoder):
    devices_all = N_GRP * N_DEV
    source_rows = sources.reshape(devices_all, PTS_DEV, R).astype(jnp.float32)
    encoder_rows = encoder.reshape(devices_all, PTS_DEV, K).astype(jnp.float32)
    coeffs = jnp.einsum('pnk,pnr->pkr', encoder_rows, source_rows).astype(jnp.bfloat16)
    for section_bit in range(BITS):
        partner = np.arange(devices_all) ^ (1 << section_bit)
        partner_coeffs = coeffs[partner]
        matrices = section_weight[:, section_bit].astype(jnp.float32)
        coeffs = (jnp.einsum('pkl,plr->pkr', matrices[:, 0], coeffs.astype(jnp.float32))
                  + jnp.einsum('pkl,plr->pkr', matrices[:, 1], partner_coeffs.astype(jnp.float32))).astype(jnp.bfloat16)
    grouped = coeffs.reshape(N_GRP, N_DEV, K, R).astype(jnp.float32)
    merged = jnp.einsum('gdhkl,hdlr->gdkr', cross_weight.astype(jnp.float32), grouped).astype(jnp.bfloat16)
    blocks = merged.reshape(devices_all, 1, K, R)
    offset = 0
    for depth_level in range(LOCAL):
        children = 2 ** (depth_level + 1)
        matrices = local_weight[:, offset:offset + children].astype(jnp.float32)
        matrices = matrices.reshape(devices_all, children // 2, 2, K, K)
        blocks = jnp.einsum('pjckl,pjlr->pjckr', matrices, blocks.astype(jnp.float32))
        blocks = blocks.reshape(devices_all, children, K, R).astype(jnp.bfloat16)
        offset = offset + children
    decoder_leaves = decoder.reshape(devices_all, 2 ** LOCAL, LEAF_T, K).astype(jnp.float32)
    target_values = jnp.einsum('pctk,pckr->pctr', decoder_leaves, blocks.astype(jnp.float32))
    return target_values.reshape(NPTS, R).astype(jnp.bfloat16)
```

```python
import functools

import jax
import jax.numpy as jnp
from jax import lax
from jax.experimental import pallas as pl
from jax.experimental.pallas import tpu as pltpu
from jax.sharding import PartitionSpec as P

LEVELS = 3
F32 = jnp.float32
BF16 = jnp.bfloat16
VMEM = pl.BlockSpec(memory_space=pltpu.VMEM)
HBM = pl.BlockSpec(memory_space=pltpu.HBM)
MIB = 1 << 20
PARTS = 2


def dot(a, b):
    return jnp.dot(a, b, preferred_element_type=F32)


def dot_first(a, b):
    return lax.dot_general(a, b, (((0,), (0,)), ((), ())), preferred_element_type=F32)


def cost(flops, moved):
    return pl.CostEstimate(flops=flops, bytes_accessed=moved, transcendentals=0)


def pieces_of(columns, shares):
    edges = [0]
    for share in shares:
        edges.append(edges[-1] + columns * share // sum(shares))
    return list(zip(edges[:-1], edges[1:]))


def partitions(columns, sections):
    first, near, far, long, last = SHARES
    shares = [first, near] + [far] * (sections - 3) + [long, last]
    return [pieces_of(columns, share) for share in shares]


def head_kernel(pieces, encoder_hbm, sources_hbm, first_ref, encoder_ref, *refs):
    near, sems = [refs[-2], *refs[:-2]], refs[-1]
    rows = encoder_ref.shape[0] // PARTS
    spans = [pl.ds(part * rows, rows) for part in range(PARTS)]

    def fetch(source, target, sem):
        copy = pltpu.make_async_copy(source, target, sem)
        copy.start()
        return copy

    lo, hi = pieces[0]
    early = []
    for part, span in enumerate(spans):
        early.append(fetch(encoder_hbm.at[span, :], encoder_ref.at[span, :], sems.at[0, part]))
        early.append(fetch(sources_hbm.at[span, pl.ds(lo, hi - lo)], near[0].at[span, :], sems.at[1, part]))
    later = [
        fetch(sources_hbm.at[:, pl.ds(lo, hi - lo)], near[i].at[:, :], sems.at[2, i])
        for i, (lo, hi) in enumerate(pieces)
        if i
    ]
    total = None
    for part, span in enumerate(spans):
        early[2 * part].wait()
        early[2 * part + 1].wait()
        term = dot_first(encoder_ref[span, :], near[0][span, :])
        total = term if total is None else total + term
    first_ref[...] = total.astype(BF16)
    for copy in later:
        copy.wait()


def encode_head(encoder, sources, pieces):
    points, size = encoder.shape
    columns = sources.shape[1]
    widths = [hi - lo for lo, hi in pieces]
    return pl.pallas_call(
        functools.partial(head_kernel, pieces),
        out_shape=[
            jax.ShapeDtypeStruct((size, widths[0]), BF16),
            jax.ShapeDtypeStruct((points, size), BF16),
            *[jax.ShapeDtypeStruct((points, width), BF16) for width in widths[1:]],
        ],
        in_specs=[HBM, HBM],
        out_specs=[VMEM] * (1 + len(widths)),
        scratch_shapes=[
            pltpu.VMEM((points, widths[0]), BF16),
            pltpu.SemaphoreType.DMA((3, max(PARTS, len(pieces)))),
        ],
        compiler_params=pltpu.CompilerParams(vmem_limit_bytes=24 * MIB),
        cost_estimate=cost(2 * points * size * widths[0], 2 * points * (size + columns)),
        name="head",
    )(
        pltpu.with_memory_space_constraint(encoder, pltpu.HBM),
        pltpu.with_memory_space_constraint(sources, pltpu.HBM),
    )


def piece_kernel(encoder_ref, sources_ref, out_ref):
    out_ref[...] = dot_first(encoder_ref[...], sources_ref[...]).astype(BF16)


def encode_piece(encoder, sources):
    points, size = encoder.shape
    width = sources.shape[1]
    return pl.pallas_call(
        piece_kernel,
        out_shape=jax.ShapeDtypeStruct((size, width), BF16),
        in_specs=[VMEM] * 2,
        out_specs=VMEM,
        compiler_params=pltpu.CompilerParams(vmem_limit_bytes=8 * MIB),
        cost_estimate=cost(2 * points * size * width, 2 * points * width),
        name="encode",
    )(encoder, sources)


def overlaps(piece, earlier):
    lo, hi = piece
    return [i for i, (a, b) in enumerate(earlier) if a < hi and b > lo]


def section_kernel(bit, piece, earlier, weight_ref, *refs):
    out_ref = refs[-1]
    lo, hi = piece
    for i, (a, b) in enumerate(earlier):
        own_ref, other_ref = refs[2 * i], refs[2 * i + 1]
        start, stop = max(a, lo), min(b, hi)
        cols = slice(start - a, stop - a)
        out_ref[:, start - lo : stop - lo] = (
            dot(weight_ref[0, bit, 0], own_ref[:, cols]) + dot(weight_ref[0, bit, 1], other_ref[:, cols])
        ).astype(BF16)


def section(weights, bit, piece, earlier, boxes):
    size = weights.shape[-1]
    width = piece[1] - piece[0]
    return pl.pallas_call(
        functools.partial(section_kernel, bit, piece, earlier),
        out_shape=jax.ShapeDtypeStruct((size, width), BF16),
        in_specs=[VMEM] * (1 + len(boxes)),
        out_specs=VMEM,
        compiler_params=pltpu.CompilerParams(vmem_limit_bytes=8 * MIB),
        cost_estimate=cost(4 * size * size * width, 1 * MIB),
        name="section",
    )(weights, *boxes)


def operator_kernel(weight_ref, decoder_ref, out_ref):
    leaf = decoder_ref.shape[0] // 2**LEVELS
    chain = [weight_ref[0, 0], weight_ref[0, 1]]
    offset = 2
    for level in range(1, LEVELS):
        children = 2 ** (level + 1)
        chain = [dot(weight_ref[0, offset + c], chain[c // 2]).astype(BF16) for c in range(children)]
        offset += children
    for c in range(2**LEVELS):
        rows = slice(c * leaf, (c + 1) * leaf)
        out_ref[rows, :] = dot(decoder_ref[rows, :], chain[c]).astype(BF16)


def local_operator(local_weight, decoder):
    points, size = decoder.shape
    return pl.pallas_call(
        operator_kernel,
        out_shape=jax.ShapeDtypeStruct((points, size), BF16),
        in_specs=[VMEM] * 2,
        out_specs=VMEM,
        compiler_params=pltpu.CompilerParams(vmem_limit_bytes=12 * MIB),
        cost_estimate=cost(2 * 20 * size**3, 4 * MIB),
        name="operator",
    )(local_weight, decoder)


TAIL_STEPS = 4


def finish_kernel(count, piece, held_piece, crossing_ref, *refs):
    boxes, operator_ref = refs[:count], refs[count]
    out_hbm, staged_ref, sems = refs[-3:]
    copies = []

    def store(source, rows, piece, sem):
        lo, hi = piece
        copies.append(pltpu.make_async_copy(source, out_hbm.at[rows, pl.ds(lo, hi - lo)], sem))
        copies[-1].start()

    if held_piece is not None:
        store(refs[count + 1], pl.ds(0, operator_ref.shape[0]), held_piece, sems.at[TAIL_STEPS])
    merged = merge(crossing_ref, boxes)
    rows = operator_ref.shape[0] // TAIL_STEPS
    for step in range(TAIL_STEPS):
        span = pl.ds(step * rows, rows)
        staged_ref[span, :] = dot(operator_ref[span, :], merged).astype(BF16)
        store(staged_ref.at[span, :], span, piece, sems.at[step])
    for copy in copies:
        copy.wait()


def merge(crossing_ref, boxes):
    total = dot(crossing_ref[0], boxes[0][...])
    for h in range(1, len(boxes)):
        total = total + dot(crossing_ref[h], boxes[h][...])
    return total.astype(BF16)


def hold_kernel(count, crossing_ref, *refs):
    refs[-1][...] = dot(refs[count][...], merge(crossing_ref, refs[:count])).astype(BF16)


def hold(crossing, boxes, operator):
    points, size = operator.shape
    width = boxes[0].shape[1]
    return pl.pallas_call(
        functools.partial(hold_kernel, len(boxes)),
        out_shape=jax.ShapeDtypeStruct((points, width), BF16),
        in_specs=[VMEM] * (2 + len(boxes)),
        out_specs=VMEM,
        compiler_params=pltpu.CompilerParams(vmem_limit_bytes=12 * MIB),
        cost_estimate=cost(2 * points * size * width, 2 * points * width),
        name="hold",
    )(crossing, *boxes, operator)


def finish(crossing, boxes, operator, piece, columns, prior, held=None, held_piece=None):
    points, size = operator.shape
    lo, hi = piece
    width = hi - lo
    operands = [crossing, *boxes, operator]
    if held is not None:
        operands.append(held)
    in_specs = [VMEM] * len(operands)
    aliases = {}
    if prior is not None:
        aliases = {len(operands): 0}
        operands.append(prior)
        in_specs.append(HBM)
    return pl.pallas_call(
        functools.partial(finish_kernel, len(boxes), piece, held_piece),
        out_shape=jax.ShapeDtypeStruct((points, columns), BF16),
        in_specs=in_specs,
        out_specs=HBM,
        scratch_shapes=[pltpu.VMEM((points, width), BF16), pltpu.SemaphoreType.DMA((TAIL_STEPS + 1,))],
        input_output_aliases=aliases,
        compiler_params=pltpu.CompilerParams(vmem_limit_bytes=12 * MIB),
        cost_estimate=cost(2 * points * size * width, 2 * points * width),
        name="finish",
    )(*operands)


def from_partner(block, axis, bit):
    count = lax.axis_size(axis)
    block = pltpu.with_memory_space_constraint(block, pltpu.VMEM)
    other = lax.ppermute(block, axis, [(i, i ^ (1 << bit)) for i in range(count)])
    return pltpu.with_memory_space_constraint(other, pltpu.VMEM)


def shards(sources, encoder, section_weight, cross_weight, local_weight, decoder):
    sections = lax.axis_size("dev").bit_length() - 1
    groups = lax.axis_size("grp")
    columns = sources.shape[1]
    plan = partitions(columns, sections)
    operator = local_operator(local_weight, decoder)
    crossing = cross_weight[0, 0]
    if groups == 2:
        me = lax.axis_index("grp")
        crossing = jnp.stack([crossing[me], crossing[1 - me]])
    first, encoder_near, *near = encode_head(encoder, sources, plan[0])
    coeffs = [first]
    for block in near:
        coeffs.append(encode_piece(encoder_near, block))
    for stage in range(sections):
        others = []
        for block in coeffs:
            others.append(from_partner(block, "dev", stage))
        mixed = []
        for piece in plan[stage + 1]:
            used = overlaps(piece, plan[stage])
            boxes = [box for j in used for box in (coeffs[j], others[j])]
            mixed.append(
                section(section_weight, stage, piece, [plan[stage][j] for j in used], boxes)
            )
        coeffs = mixed
    out = None
    arrived = []
    for block in coeffs:
        if groups == 2:
            arrived.append([block, from_partner(block, "grp", 0)])
        else:
            every = lax.all_gather(block, "grp")
            arrived.append([every[h] for h in range(groups)])
    held = held_piece = None
    for i, (piece, boxes) in enumerate(zip(plan[sections], arrived)):
        if i and i == len(arrived) - 2:
            held, held_piece = hold(crossing, boxes, operator), piece
        else:
            out = finish(crossing, boxes, operator, piece, columns, out, held, held_piece)
    return out


SHARES = ((1, 5), (1, 2, 3), (1, 2, 2, 1), (1, 2, 2, 1), (1, 2, 2, 1))


def solution(mesh):
    placed = (
        P(("grp", "dev"), None),
        P(("grp", "dev"), None),
        P(("grp", "dev"), None, None, None, None),
        P("grp", "dev", None, None, None),
        P(("grp", "dev"), None, None, None),
        P(("grp", "dev"), None),
    )
    return jax.shard_map(
        shards, mesh=mesh, in_specs=placed, out_specs=P(("grp", "dev"), None), check_vma=False
    )
```

```python
import functools

import jax
import jax.numpy as jnp
from jax import lax
from jax.experimental import pallas as pl
from jax.experimental.pallas import tpu as pltpu
from jax.sharding import PartitionSpec as P

LEVELS = 3
F32 = jnp.float32
BF16 = jnp.bfloat16
VMEM = pl.BlockSpec(memory_space=pltpu.VMEM)
HBM = pl.BlockSpec(memory_space=pltpu.HBM)
MIB = 1 << 20
PARTS = 2


def dot(a, b):
    return jnp.dot(a, b, preferred_element_type=F32)


def dot_first(a, b):
    return lax.dot_general(a, b, (((0,), (0,)), ((), ())), preferred_element_type=F32)


def cost(flops, moved):
    return pl.CostEstimate(flops=flops, bytes_accessed=moved, transcendentals=0)


def pieces_of(columns, shares):
    edges = [0]
    for share in shares:
        edges.append(edges[-1] + columns * share // sum(shares))
    return list(zip(edges[:-1], edges[1:]))


def partitions(columns, sections):
    first, near, far, long, last = SHARES
    shares = [first, near] + [far] * (sections - 3) + [long, last]
    return [pieces_of(columns, share) for share in shares]


def head_kernel(pieces, encoder_hbm, sources_hbm, first_ref, encoder_ref, *refs):
    near, sems = [refs[-2], *refs[:-2]], refs[-1]
    rows = encoder_ref.shape[0] // PARTS
    spans = [pl.ds(part * rows, rows) for part in range(PARTS)]

    def fetch(source, target, sem):
        copy = pltpu.make_async_copy(source, target, sem)
        copy.start()
        return copy

    lo, hi = pieces[0]
    early = []
    for part, span in enumerate(spans):
        early.append(fetch(encoder_hbm.at[span, :], encoder_ref.at[span, :], sems.at[0, part]))
        early.append(fetch(sources_hbm.at[span, pl.ds(lo, hi - lo)], near[0].at[span, :], sems.at[1, part]))
    later = [
        fetch(
            sources_hbm.at[pl.ds(half * (rows * PARTS // 2), rows * PARTS // 2), pl.ds(lo, hi - lo)],
            near[i].at[pl.ds(half * (rows * PARTS // 2), rows * PARTS // 2), :],
            sems.at[2, 2 * i - 2 + half],
        )
        for i, (lo, hi) in enumerate(pieces)
        if i
        for half in range(2)
    ]
    total = None
    for part, span in enumerate(spans):
        early[2 * part].wait()
        early[2 * part + 1].wait()
        term = dot_first(encoder_ref[span, :], near[0][span, :])
        total = term if total is None else total + term
    first_ref[...] = total.astype(BF16)
    for copy in later:
        copy.wait()


def encode_head(encoder, sources, pieces):
    points, size = encoder.shape
    columns = sources.shape[1]
    widths = [hi - lo for lo, hi in pieces]
    return pl.pallas_call(
        functools.partial(head_kernel, pieces),
        out_shape=[
            jax.ShapeDtypeStruct((size, widths[0]), BF16),
            jax.ShapeDtypeStruct((points, size), BF16),
            *[jax.ShapeDtypeStruct((points, width), BF16) for width in widths[1:]],
        ],
        in_specs=[HBM, HBM],
        out_specs=[VMEM] * (1 + len(widths)),
        scratch_shapes=[
            pltpu.VMEM((points, widths[0]), BF16),
            pltpu.SemaphoreType.DMA((3, max(PARTS, 2 * len(pieces)))),
        ],
        compiler_params=pltpu.CompilerParams(vmem_limit_bytes=24 * MIB),
        cost_estimate=cost(2 * points * size * widths[0], 2 * points * (size + columns)),
        name="head",
    )(
        pltpu.with_memory_space_constraint(encoder, pltpu.HBM),
        pltpu.with_memory_space_constraint(sources, pltpu.HBM),
    )


def piece_kernel(encoder_ref, sources_ref, out_ref):
    out_ref[...] = dot_first(encoder_ref[...], sources_ref[...]).astype(BF16)


def encode_piece(encoder, sources):
    points, size = encoder.shape
    width = sources.shape[1]
    return pl.pallas_call(
        piece_kernel,
        out_shape=jax.ShapeDtypeStruct((size, width), BF16),
        in_specs=[VMEM] * 2,
        out_specs=VMEM,
        compiler_params=pltpu.CompilerParams(vmem_limit_bytes=8 * MIB),
        cost_estimate=cost(2 * points * size * width, 2 * points * width),
        name="encode",
    )(encoder, sources)


def overlaps(piece, earlier):
    lo, hi = piece
    return [i for i, (a, b) in enumerate(earlier) if a < hi and b > lo]


def section_kernel(bit, piece, earlier, weight_ref, *refs):
    out_ref = refs[-1]
    lo, hi = piece
    for i, (a, b) in enumerate(earlier):
        own_ref, other_ref = refs[2 * i], refs[2 * i + 1]
        start, stop = max(a, lo), min(b, hi)
        cols = slice(start - a, stop - a)
        out_ref[:, start - lo : stop - lo] = (
            dot(weight_ref[0, bit, 0], own_ref[:, cols]) + dot(weight_ref[0, bit, 1], other_ref[:, cols])
        ).astype(BF16)


def section(weights, bit, piece, earlier, boxes):
    size = weights.shape[-1]
    width = piece[1] - piece[0]
    return pl.pallas_call(
        functools.partial(section_kernel, bit, piece, earlier),
        out_shape=jax.ShapeDtypeStruct((size, width), BF16),
        in_specs=[VMEM] * (1 + len(boxes)),
        out_specs=VMEM,
        compiler_params=pltpu.CompilerParams(vmem_limit_bytes=8 * MIB),
        cost_estimate=cost(4 * size * size * width, 1 * MIB),
        name="section",
    )(weights, *boxes)


def operator_kernel(weight_ref, decoder_ref, out_ref):
    leaf = decoder_ref.shape[0] // 2**LEVELS
    chain = [weight_ref[0, 0], weight_ref[0, 1]]
    offset = 2
    for level in range(1, LEVELS):
        children = 2 ** (level + 1)
        chain = [dot(weight_ref[0, offset + c], chain[c // 2]).astype(BF16) for c in range(children)]
        offset += children
    for c in range(2**LEVELS):
        rows = slice(c * leaf, (c + 1) * leaf)
        out_ref[rows, :] = dot(decoder_ref[rows, :], chain[c]).astype(BF16)


def local_operator(local_weight, decoder):
    points, size = decoder.shape
    return pl.pallas_call(
        operator_kernel,
        out_shape=jax.ShapeDtypeStruct((points, size), BF16),
        in_specs=[VMEM] * 2,
        out_specs=VMEM,
        compiler_params=pltpu.CompilerParams(vmem_limit_bytes=12 * MIB),
        cost_estimate=cost(2 * 20 * size**3, 4 * MIB),
        name="operator",
    )(local_weight, decoder)


TAIL_STEPS = 4


def finish_kernel(count, piece, held_piece, crossing_ref, *refs):
    boxes, operator_ref = refs[:count], refs[count]
    out_hbm, staged_ref, sems = refs[-3:]
    copies = []

    def store(source, rows, piece, sem):
        lo, hi = piece
        copies.append(pltpu.make_async_copy(source, out_hbm.at[rows, pl.ds(lo, hi - lo)], sem))
        copies[-1].start()

    if held_piece is not None:
        store(refs[count + 1], pl.ds(0, operator_ref.shape[0]), held_piece, sems.at[TAIL_STEPS])
    merged = merge(crossing_ref, boxes)
    rows = operator_ref.shape[0] // TAIL_STEPS
    for step in range(TAIL_STEPS):
        span = pl.ds(step * rows, rows)
        staged_ref[span, :] = dot(operator_ref[span, :], merged).astype(BF16)
        store(staged_ref.at[span, :], span, piece, sems.at[step])
    for copy in copies:
        copy.wait()


def merge(crossing_ref, boxes):
    total = dot(crossing_ref[0], boxes[0][...])
    for h in range(1, len(boxes)):
        total = total + dot(crossing_ref[h], boxes[h][...])
    return total.astype(BF16)


def hold_kernel(count, crossing_ref, *refs):
    refs[-1][...] = dot(refs[count][...], merge(crossing_ref, refs[:count])).astype(BF16)


def hold(crossing, boxes, operator):
    points, size = operator.shape
    width = boxes[0].shape[1]
    return pl.pallas_call(
        functools.partial(hold_kernel, len(boxes)),
        out_shape=jax.ShapeDtypeStruct((points, width), BF16),
        in_specs=[VMEM] * (2 + len(boxes)),
        out_specs=VMEM,
        compiler_params=pltpu.CompilerParams(vmem_limit_bytes=12 * MIB),
        cost_estimate=cost(2 * points * size * width, 2 * points * width),
        name="hold",
    )(crossing, *boxes, operator)


def finish(crossing, boxes, operator, piece, columns, prior, held=None, held_piece=None):
    points, size = operator.shape
    lo, hi = piece
    width = hi - lo
    operands = [crossing, *boxes, operator]
    if held is not None:
        operands.append(held)
    in_specs = [VMEM] * len(operands)
    aliases = {}
    if prior is not None:
        aliases = {len(operands): 0}
        operands.append(prior)
        in_specs.append(HBM)
    return pl.pallas_call(
        functools.partial(finish_kernel, len(boxes), piece, held_piece),
        out_shape=jax.ShapeDtypeStruct((points, columns), BF16),
        in_specs=in_specs,
        out_specs=HBM,
        scratch_shapes=[pltpu.VMEM((points, width), BF16), pltpu.SemaphoreType.DMA((TAIL_STEPS + 1,))],
        input_output_aliases=aliases,
        compiler_params=pltpu.CompilerParams(vmem_limit_bytes=12 * MIB),
        cost_estimate=cost(2 * points * size * width, 2 * points * width),
        name="finish",
    )(*operands)


def from_partner(block, axis, bit):
    count = lax.axis_size(axis)
    block = pltpu.with_memory_space_constraint(block, pltpu.VMEM)
    other = lax.ppermute(block, axis, [(i, i ^ (1 << bit)) for i in range(count)])
    return pltpu.with_memory_space_constraint(other, pltpu.VMEM)


def shards(sources, encoder, section_weight, cross_weight, local_weight, decoder):
    sections = lax.axis_size("dev").bit_length() - 1
    groups = lax.axis_size("grp")
    columns = sources.shape[1]
    plan = partitions(columns, sections)
    operator = local_operator(local_weight, decoder)
    crossing = cross_weight[0, 0]
    if groups == 2:
        me = lax.axis_index("grp")
        crossing = jnp.stack([crossing[me], crossing[1 - me]])
    first, encoder_near, *near = encode_head(encoder, sources, plan[0])
    coeffs = [first]
    for block in near:
        coeffs.append(encode_piece(encoder_near, block))
    for stage in range(sections):
        others = []
        for block in coeffs:
            others.append(from_partner(block, "dev", stage))
        mixed = []
        for piece in plan[stage + 1]:
            used = overlaps(piece, plan[stage])
            boxes = [box for j in used for box in (coeffs[j], others[j])]
            mixed.append(
                section(section_weight, stage, piece, [plan[stage][j] for j in used], boxes)
            )
        coeffs = mixed
    out = None
    arrived = []
    for block in coeffs:
        if groups == 2:
            arrived.append([block, from_partner(block, "grp", 0)])
        else:
            every = lax.all_gather(block, "grp")
            arrived.append([every[h] for h in range(groups)])
    held = held_piece = None
    for i, (piece, boxes) in enumerate(zip(plan[sections], arrived)):
        if i and i == len(arrived) - 2:
            held, held_piece = hold(crossing, boxes, operator), piece
        else:
            out = finish(crossing, boxes, operator, piece, columns, out, held, held_piece)
    return out


SHARES = ((1, 5), (1, 2, 3), (1, 2, 2, 1), (1, 2, 2, 1), (1, 2, 2, 1))


def solution(mesh):
    placed = (
        P(("grp", "dev"), None),
        P(("grp", "dev"), None),
        P(("grp", "dev"), None, None, None, None),
        P("grp", "dev", None, None, None),
        P(("grp", "dev"), None, None, None),
        P(("grp", "dev"), None),
    )
    return jax.shard_map(
        shards, mesh=mesh, in_specs=placed, out_specs=P(("grp", "dev"), None), check_vma=False
    )
```
